256 devices in a mesh: node: 64 (over x, z, core), local: 4 (over y).
Axes of the slice: x: 4, y: 4, z: 8, core: 2. Of those that a mesh axis runs over, the one named last changes fastest.
Arguments:
- tokens: bfloat16 [1024, 7168], P(('node', 'local')), may hold values from -6 to 6
- expert_ids: int32 [1024, 8], P(('node', 'local')), may hold values from 0 to 63, as said below
- combine_fixed: int32 [1024, 8], P(('node', 'local')), may hold values from 1 to 65535
- gate_weight: bfloat16 [64, 7168, 1024], P('node', None, 'local'), may hold values from -0.0625 to 0.0625
- up_weight: bfloat16 [64, 7168, 1024], P('node', None, 'local'), may hold values from -0.0625 to 0.0625
- down_weight: bfloat16 [64, 1024, 7168], P('node', None, 'local'), may hold values from -0.1875 to 0.1875
Outputs:
- mixed: bfloat16 [1024, 7168], P(('node', 'local'))
The draws below stay inside these ranges and needn't reach their ends.
Inputs may be any that keep to these rules, and one draw needn't show every extreme that they name: `expert_ids`: each row names 8 different experts. Among the 4 rows of one device no expert is named more than 2 times, and one expert, the same for every device, is named exactly 2 times by the rows of every device. Other experts may also be named 2 times by the rows of some devices.
All inputs are finite; a program needn't handle non-finite values.
Results may differ from the reference program's by a relative error of at most 0.0057.
Values may be sent and summed in bfloat16 or wider, within the bound.
No kernel may reach another device: no remote copies, remote signals or barrier semaphores. Data moves between devices by JAX's collectives and lax.ppermute only.
A program may use at most 128 MiB of HBM per device.

```python
import jax
import jax.numpy as jnp
from jax import lax

D = 7168
H_WIN = 1024
TOPK = 8
TOK_DEV = 4
EXPERTS = 64
CAP = 2
TOKENS = 1024
MAXR = 512


def draw_expert_ids(key, part):
    key_hot, key_blocks = jax.random.split(jax.random.fold_in(key, 17))
    favored = jax.random.randint(key_hot, (), 0, EXPERTS)
    block_count = TOKENS // TOK_DEV
    window = TOPK if TOK_DEV > CAP else TOPK - 1
    filled = TOK_DEV * TOPK - CAP
    shortest = max(window, (filled + CAP - 1) // CAP)

    def one_block(block_key):
        key_perm, key_cols, key_rows, key_len = jax.random.split(block_key, 4)
        others = jax.random.permutation(key_perm, EXPERTS - 1)
        others = others + (others >= favored).astype(jnp.int32)
        cycle = jax.random.randint(key_len, (), shortest, EXPERTS)
        row_index = jnp.arange(TOK_DEV, dtype=jnp.int32)
        has_favored = (row_index < CAP).astype(jnp.int32)
        begin = row_index * TOPK - jnp.minimum(row_index, CAP)
        column = jnp.arange(TOPK, dtype=jnp.int32)
        position = (begin[:, None] + column[None, :] - has_favored[:, None]) % cycle
        grid = jnp.where((has_favored[:, None] == 1) & (column[None, :] == 0), favored, others[position])
        scores = jax.random.randint(key_cols, (TOK_DEV, TOPK), 0, 1024) * TOPK + column[None, :]
        shuffle = jnp.argsort(scores, axis=1)
        grid = jnp.take_along_axis(grid, shuffle, axis=1)
        grid = grid[jax.random.permutation(key_rows, TOK_DEV)]
        return grid
    block_keys = jax.random.split(key_blocks, block_count)
    return jax.vmap(one_block)(block_keys).reshape(TOKENS, TOPK).astype(jnp.int32)


def set_ends(drawn, rng, least, largest):
    dims = drawn.shape
    spot = [jax.random.randint(jax.random.fold_in(rng, axis), (), 0, dims[axis]) for axis in range(len(dims))]
    drawn = drawn.at[tuple(spot)].set(least)
    longest = dims.index(max(dims))
    spot[longest] = (spot[longest] + 1) % dims[longest]
    return drawn.at[tuple(spot)].set(largest)


def block_levels(rng, shape, cuts, low, largest):
    def one(axis_at, shards_of):
        heights = jax.random.uniform(jax.random.fold_in(jax.random.fold_in(rng, 6), axis_at), (shards_of,), jnp.float32, low / len(cuts), largest / len(cuts))
        return jnp.repeat(jnp.exp(heights), shape[axis_at] // shards_of).reshape((-1,) + (1,) * (len(shape) - axis_at - 1))

    gain = one(*cuts[0])
    for cut in cuts[1:]:
        gain = gain * one(*cut)
    return gain


def gaussian(key, shape, deviation, bound, shards=(), kind=jnp.bfloat16):
    loudness = block_levels(key, shape, shards, -0.22, 0.18) if shards else 1.0
    values = jax.random.normal(key, shape, jnp.float32) * deviation * loudness
    return jnp.minimum(jnp.maximum(values, -bound), bound).astype(kind)


def setup_inputs(seed: int = 0) -> dict:
    key_list = jax.random.split(jax.random.key(seed), 7)
    return {
        "tokens": gaussian(key_list[0], (TOKENS, D), 1.0, 6.0, ((0, 256),)),
        "expert_ids": draw_expert_ids(jax.random.fold_in(key_list[6], 71), 0),
        "combine_fixed": set_ends(jax.random.randint(key_list[2], (TOKENS, TOPK), 1, 65536), jax.random.fold_in(key_list[2], 1), 1, 65535).astype(jnp.int32),
        "gate_weight": gaussian(key_list[3], (EXPERTS, D, H_WIN), D ** -0.5, 0.0625, ((0, 64), (2, 4))),
        "up_weight": gaussian(key_list[4], (EXPERTS, D, H_WIN), D ** -0.5, 0.0625, ((0, 64), (2, 4))),
        "down_weight": gaussian(key_list[5], (EXPERTS, H_WIN, D), H_WIN ** -0.5, 0.1875, ((0, 64), (2, 4))),
    }


def reference(tokens, expert_ids, combine_fixed, gate_weight, up_weight, down_weight):
    pairs = TOKENS * TOPK
    flat_experts = expert_ids.reshape(-1).astype(jnp.int32)
    order = jnp.argsort(flat_experts * pairs + jnp.arange(pairs, dtype=jnp.int32)).astype(jnp.int32)
    counts = jnp.sum((flat_experts[:, None] == jnp.arange(EXPERTS, dtype=jnp.int32)[None, :]).astype(jnp.int32), axis=0)
    starts = (jnp.cumsum(counts) - counts).astype(jnp.int32)
    padded_order = jnp.concatenate([order, jnp.zeros((MAXR,), jnp.int32)])
    weights = combine_fixed.reshape(-1).astype(jnp.float32) / 32768.0
    block = min(128, MAXR)
    blocks = MAXR // block

    def per_expert(expert, total):
        first = starts[expert]
        count = counts[expert]
        w_gate = gate_weight[expert]
        w_up = up_weight[expert]
        w_down = down_weight[expert]

        def per_block(index, total):
            def work(total):
                picked = lax.dynamic_slice(padded_order, (first + index * block,), (block,))
                live = (index * block + jnp.arange(block, dtype=jnp.int32)) < count
                token_row = (picked // TOPK).astype(jnp.int32)
                rows_in = tokens[token_row]
                gate = jnp.dot(rows_in, w_gate, preferred_element_type=jnp.float32)
                upper = jnp.dot(rows_in, w_up, preferred_element_type=jnp.float32)
                hidden = (jax.nn.silu(gate) * upper).astype(jnp.bfloat16)
                summed = jnp.dot(hidden, w_down, preferred_element_type=jnp.float32)
                result = lax.optimization_barrier(summed.astype(jnp.bfloat16)).astype(jnp.float32)
                scale = jnp.where(live, weights[picked], jnp.zeros((block,), jnp.float32))
                return total.at[token_row].add(scale[:, None] * result)

            return lax.cond(index * block < count, work, lambda carry: carry, total)

        return lax.fori_loop(0, blocks, per_block, total)

    mixed = lax.fori_loop(0, EXPERTS, per_expert, jnp.zeros((TOKENS, D), jnp.float32))
    return mixed.astype(jnp.bfloat16)
```

```python
import jax
import jax.numpy as jnp
from jax import lax
from jax.sharding import Mesh, PartitionSpec as P

NX, NZ, NC, NY = 4, 8, 2, 4
META = 128


def shift(v, axis, size, step):
    return lax.ppermute(v, axis, [(i, (i + step) % size) for i in range(size)])


def shards(tokens, expert_ids, combine_fixed, gate_weight, up_weight, down_weight):
    rows, width = tokens.shape
    chosen = expert_ids.shape[1]
    bf16, f32 = jnp.bfloat16, jnp.float32
    w_gate, w_up, w_down = gate_weight[0], up_weight[0], down_weight[0]
    slice_h = w_gate.shape[1]
    slice_d = w_down.shape[1]
    me_y = lax.axis_index("local")
    me_expert = lax.axis_index(("x", "z", "core"))

    meta = jnp.concatenate([expert_ids, combine_fixed // 256, combine_fixed % 256], axis=1).astype(bf16)
    meta = jnp.pad(meta, ((0, 0), (0, META - 3 * chosen)))
    payload = jnp.concatenate([tokens, meta], axis=1)
    node_rows = lax.all_to_all(
        jnp.broadcast_to(payload[None], (NY,) + payload.shape), "local", 0, 0, tiled=True
    ).reshape(NY * rows, width + META)
    block = node_rows.shape[0]

    plane = jnp.concatenate([node_rows] + [shift(node_rows, "x", NX, -k) for k in range(1, NX)], axis=0)
    ahead, behind = {0: plane}, {0: plane}
    for s in range(1, NZ // 2 + 1):
        ahead[s] = shift(ahead[s - 1], "z", NZ, -1)
        if s < NZ // 2:
            behind[s] = shift(behind[s - 1], "z", NZ, 1)
    own = [ahead[s] for s in range(NZ // 2 + 1)] + [behind[s] for s in range(NZ // 2 - 1, 0, -1)]
    other = [shift(v, "core", NC, 1) for v in own]

    w_down = jnp.concatenate([w_down, w_down], axis=0)
    w_down = lax.dynamic_slice(w_down, (me_y * slice_h, 0), (NY * slice_h, slice_d))

    groups = [(0, 1, 7), (2, 6), (3, 4, 5)]
    parts = {}
    for group in groups:
        flat = jnp.concatenate([side[j] for side in (own, other) for j in group], axis=0)
        gate = jnp.dot(flat[:, :width], w_gate, preferred_element_type=f32)
        upper = jnp.dot(flat[:, :width], w_up, preferred_element_type=f32)
        hidden = (jax.nn.silu(gate) * upper).astype(bf16)
        full = jnp.concatenate([hidden] + [shift(hidden, "local", NY, -k) for k in range(1, NY)], axis=1)
        made = jnp.dot(full, w_down, preferred_element_type=f32).astype(bf16).astype(f32)
        info = flat[:, width:].astype(f32)
        ids = info[:, :chosen].astype(jnp.int32)
        fixed = info[:, chosen : 2 * chosen] * 256.0 + info[:, 2 * chosen : 3 * chosen]
        scale = jnp.sum(jnp.where(ids == me_expert, fixed, 0.0), axis=1) / 32768.0
        made = (made * scale[:, None]).reshape(2, len(group), NX, block, slice_d)
        mine = made[0] + shift(made[1].astype(bf16), "core", NC, 1).astype(f32)
        total = mine[:, 0]
        for k in range(1, NX):
            total = total + shift(mine[:, k].astype(bf16), "x", NX, k).astype(f32)
        for i, j in enumerate(group):
            parts[j] = total[i]
    result = parts[0]
    for j in range(1, NZ):
        result = result + shift(parts[j].astype(bf16), "z", NZ, j).astype(f32)
    result = result.astype(bf16)
    return lax.all_to_all(result, "local", split_axis=0, concat_axis=1, tiled=True)


def solution(mesh):
    fine = Mesh(mesh.devices.reshape(NX, NZ, NC, NY), ("x", "z", "core", "local"))
    node = ("x", "z", "core")
    row = P(node + ("local",), None)
    wide = P(node, None, "local")
    return jax.shard_map(
        shards, mesh=fine, in_specs=(row, row, row, wide, wide, wide), out_specs=row, check_vma=False
    )
```

```python
import jax
import jax.numpy as jnp
from jax import lax
from jax.sharding import Mesh, PartitionSpec as P


NX, NZ, NC, NY = 4, 8, 2, 4
META = 128
Z_ORDER = (0, 4, 1, 5, 7, 3, 2, 6)


def shift(v, axis, step):
    size = lax.axis_size(axis)
    return lax.ppermute(v, axis, [(i, (i + step) % size) for i in range(size)])


def layer(tokens, expert_ids, combine_fixed, gate_weight, up_weight, down_weight):
    rows, width = tokens.shape
    chosen = expert_ids.shape[1]
    bf16, f32 = jnp.bfloat16, jnp.float32
    w_gate, w_up, w_down = gate_weight[0], up_weight[0], down_weight[0]
    slice_h = w_gate.shape[1]
    slice_d = w_down.shape[1]
    half = width // NC
    cols = half + META
    me_y, me_z, me_c = lax.axis_index("local"), lax.axis_index("z"), lax.axis_index("core")
    me_expert = lax.axis_index(("x", "z", "core"))

    meta = jnp.concatenate([expert_ids, combine_fixed // 256, combine_fixed % 256], axis=1).astype(bf16)
    meta = jnp.pad(meta, ((0, 0), (0, META - 3 * chosen)))
    payload = jnp.stack(
        [jnp.concatenate([tokens[:, c * half : (c + 1) * half], meta], axis=1) for c in range(NC)]
    )
    payload = jnp.broadcast_to(payload[:, None], (NC, NY, rows, cols)).reshape(NC * NY, rows, cols)
    block = lax.all_to_all(payload, ("core", "local"), 0, 0, tiled=True)
    block = block.reshape(NC * NY, 2, rows // 2, cols).transpose(1, 0, 2, 3).reshape(-1, cols)
    b = block.shape[0] // 2
    far = shift(block, "z", -4)

    pair = lax.optimization_barrier(jnp.concatenate([block[:b], far[:b]], axis=0))
    up, down = shift(pair, "z", -1), shift(pair, "z", 1)
    up2, down2 = shift(up[:b], "z", -1), shift(down[:b], "z", 1)
    x0 = jnp.concatenate([pair, up, down, up2, down2], axis=0)
    x1, x3 = shift(x0, "x", -1), shift(x0, "x", 1)
    x2 = [shift(x1[: 4 * b], "x", -1), shift(x3[4 * b :], "x", 1)]

    pair = lax.optimization_barrier(jnp.concatenate([block[b:], far[b:]], axis=0))
    z0 = jnp.concatenate([pair] + [shift(pair, "x", -k) for k in range(1, NX)], axis=0)
    z1, z7 = shift(z0, "z", -1), shift(z0, "z", 1)
    z2 = [shift(z1[: 4 * b], "z", -1), shift(z7[4 * b :], "z", 1)]

    def half_of(w, c):
        return lax.dynamic_slice(w, (c * half, 0), (half, slice_h))

    theirs = jnp.concatenate([half_of(w_gate, 1 - me_c), half_of(w_up, 1 - me_c)], axis=1)
    theirs = shift(theirs, "core", 1)
    w_both = jnp.concatenate([half_of(w_gate, me_c), half_of(w_up, me_c), theirs], axis=1)
    w_down_rel = jnp.concatenate([w_down, w_down], axis=0)
    w_down_rel = lax.dynamic_slice(w_down_rel, (me_y * slice_h, 0), (NY * slice_h, slice_d))

    done = {}
    for colour, pieces in [("second", [z0, z1, z7] + z2), ("first", [x0, x1, x3] + x2)]:
        flat = jnp.concatenate(pieces, axis=0)
        made = jnp.dot(flat[:, :half], w_both, preferred_element_type=f32)
        other = shift(made[:, 2 * slice_h :], "core", 1)
        made = made[:, : 2 * slice_h] + other
        hidden = (jax.nn.silu(made[:, :slice_h]) * made[:, slice_h:]).astype(bf16)
        full = [hidden] + [shift(hidden, "local", -y) for y in range(1, NY)]
        out = jnp.dot(jnp.concatenate(full, axis=1), w_down_rel, preferred_element_type=f32)
        out = out.astype(bf16).astype(f32)
        info = flat[:, half:].astype(f32)
        ids = info[:, :chosen].astype(jnp.int32)
        fixed = info[:, chosen : 2 * chosen] * 256.0 + info[:, 2 * chosen : 3 * chosen]
        scale = jnp.sum(jnp.where(ids == me_expert, fixed, 0.0), axis=1) / 32768.0
        out = (out * scale[:, None]).astype(bf16).reshape(-1, NC, b // NC, slice_d)
        mine = lax.dynamic_index_in_dim(out, me_c, 1, keepdims=False)
        away = lax.dynamic_index_in_dim(out, 1 - me_c, 1, keepdims=False)
        out = (mine.astype(f32) + shift(away, "core", 1).astype(f32)).astype(bf16)
        if colour == "first":
            part = {k: out[j * NZ : (j + 1) * NZ] for j, k in enumerate((0, 1, 3, 2))}
        else:
            near = out[: 3 * NZ].reshape((3, NX, 2) + out.shape[1:])
            last = out[3 * NZ :].reshape((NX, 2) + out.shape[1:])
            part = {
                k: jnp.concatenate([near[0, k], near[1, k], near[2, k], last[k] if k < 2 else last[k][::-1]])
                for k in range(NX)
            }
        total = part[0].astype(f32)
        for k in range(1, NX):
            total = total + shift(part[k], "x", k).astype(f32)
        done[colour] = total.astype(bf16)
    wanted = (jnp.arange(NZ, dtype=jnp.int32) - me_z) % NZ
    pick = (jnp.array(Z_ORDER, jnp.int32)[None, :] == wanted[:, None])[:, :, None, None, None]
    ring = jnp.stack([v.reshape(NZ, NY, rows // 2, slice_d) for v in (done["first"], done["second"])], axis=2)
    ring = ring.reshape(NZ, NY, rows, slice_d)
    ring = jnp.sum(jnp.where(pick, ring.astype(f32)[None], 0.0), axis=1).astype(bf16)
    ring = lax.all_to_all(ring.reshape(NZ * NY, rows, slice_d), ("z", "local"), 0, 0, tiled=True)
    mixed = jnp.sum(ring.reshape(NZ, NY, rows, slice_d).astype(f32), axis=0).astype(bf16)
    return jnp.concatenate([mixed[d] for d in range(NY)], axis=1)


def solution(mesh):
    fine = Mesh(mesh.devices.reshape(NX, NZ, NC, NY), ("x", "z", "core", "local"))
    node = ("x", "z", "core")
    row = P(node + ("local",), None)
    wide = P(node, None, "local")
    return jax.shard_map(layer, mesh=fine, in_specs=(row, row, row, wide, wide, wide), out_specs=row, check_vma=False)
```

```python
import jax
import jax.numpy as jnp
from jax import lax
from jax.experimental import pallas as pl
from jax.experimental.pallas import tpu as pltpu
from jax.sharding import Mesh, PartitionSpec as P


NX, NZ, NC, NY = 4, 8, 2, 4
META = 128
Z_ORDER = (0, 4, 1, 5, 7, 3, 2, 6)


def shift(v, axis, step):
    size = lax.axis_size(axis)
    return lax.ppermute(v, axis, [(i, (i + step) % size) for i in range(size)])


def roll_kernel(me_ref, w_ref, out_ref):
    out_ref[...] = w_ref[...]


def roll_rows(me, w):
    block = (w.shape[0] // NY, w.shape[1])
    return pl.pallas_call(
        roll_kernel,
        out_shape=jax.ShapeDtypeStruct(w.shape, w.dtype),
        grid_spec=pltpu.PrefetchScalarGridSpec(
            num_scalar_prefetch=1,
            grid=(NY,),
            in_specs=[pl.BlockSpec(block, lambda n, me: (lax.rem(n + me[0], NY), 0))],
            out_specs=pl.BlockSpec(block, lambda n, me: (n, 0)),
        ),
        compiler_params=pltpu.CompilerParams(vmem_limit_bytes=6 << 20),
    )(me, w)


def place_kernel(me_ref, table_ref, x_ref, recv_ref, out_ref):
    def one(n, carry):
        k = lax.rem(n // NZ + NX - me_ref[0], NX)
        j = lax.rem(lax.rem(n, NZ) + NZ - me_ref[1], NZ)
        source = table_ref[k * NZ + j]
        mine = x_ref[source, me_ref[2]].astype(jnp.float32)
        out_ref[n] = (mine + recv_ref[source].astype(jnp.float32)).astype(jnp.bfloat16)
        return carry

    lax.fori_loop(0, NX * NZ, one, 0)


def place_blocks(me, table, x, recv):
    return pl.pallas_call(
        place_kernel,
        out_shape=jax.ShapeDtypeStruct(recv.shape, recv.dtype),
        grid_spec=pltpu.PrefetchScalarGridSpec(
            num_scalar_prefetch=2,
            grid=(1,),
            in_specs=[
                pl.BlockSpec(x.shape, lambda n, me, table: (0, 0, 0, 0)),
                pl.BlockSpec(recv.shape, lambda n, me, table: (0, 0, 0)),
            ],
            out_specs=pl.BlockSpec(recv.shape, lambda n, me, table: (0, 0, 0)),
        ),
        compiler_params=pltpu.CompilerParams(vmem_limit_bytes=20 << 20),
    )(me, table, x, recv)


FIRST = [(0, 1, 3, 2)[k] * NZ + Z_ORDER.index(j) for k in range(NX) for j in range(NZ)]
SECOND = [
    (Z_ORDER.index(j) // 2) * 8 + k * 2 + (Z_ORDER.index(j) % 2 if k < 2 or j not in (2, 6) else 1 - Z_ORDER.index(j) % 2)
    for k in range(NX)
    for j in range(NZ)
]


def layer(tokens, expert_ids, combine_fixed, gate_weight, up_weight, down_weight):
    rows, width = tokens.shape
    chosen = expert_ids.shape[1]
    bf16, f32 = jnp.bfloat16, jnp.float32
    w_gate, w_up, w_down = gate_weight[0], up_weight[0], down_weight[0]
    slice_h = w_gate.shape[1]
    slice_d = w_down.shape[1]
    half = width // NC
    cols = half + META
    me_y, me_z, me_c = lax.axis_index("local"), lax.axis_index("z"), lax.axis_index("core")
    me_expert = lax.axis_index(("x", "z", "core"))

    meta = jnp.concatenate([expert_ids, combine_fixed // 256, combine_fixed % 256], axis=1).astype(bf16)
    meta = jnp.pad(meta, ((0, 0), (0, META - 3 * chosen)))
    payload = jnp.stack(
        [jnp.concatenate([tokens[:, c * half : (c + 1) * half], meta], axis=1) for c in range(NC)]
    )
    payload = jnp.broadcast_to(payload[:, None], (NC, NY, rows, cols)).reshape(NC * NY, rows, cols)
    block = lax.all_to_all(payload, ("core", "local"), 0, 0, tiled=True)
    block = block.reshape(NC * NY, 2, rows // 2, cols).transpose(1, 0, 2, 3).reshape(-1, cols)
    b = block.shape[0] // 2
    far = shift(block, "z", -4)

    pair = lax.optimization_barrier(jnp.concatenate([block[:b], far[:b]], axis=0))
    up, down = shift(pair, "z", -1), shift(pair, "z", 1)
    up2, down2 = shift(up[:b], "z", -1), shift(down[:b], "z", 1)
    x0 = jnp.concatenate([pair, up, down, up2, down2], axis=0)
    x1, x3 = shift(x0, "x", -1), shift(x0, "x", 1)
    x2 = [shift(x1[: 4 * b], "x", -1), shift(x3[4 * b :], "x", 1)]

    pair = lax.optimization_barrier(jnp.concatenate([block[b:], far[b:]], axis=0))
    z0 = jnp.concatenate([pair] + [shift(pair, "x", -k) for k in range(1, NX)], axis=0)
    z1, z7 = shift(z0, "z", -1), shift(z0, "z", 1)
    z2 = [shift(z1[: 4 * b], "z", -1), shift(z7[4 * b :], "z", 1)]

    def half_of(w, c):
        return lax.dynamic_slice(w, (c * half, 0), (half, slice_h))

    theirs = jnp.concatenate([half_of(w_gate, 1 - me_c), half_of(w_up, 1 - me_c)], axis=1)
    theirs = shift(theirs, "core", 1)
    w_both = jnp.concatenate([half_of(w_gate, me_c), half_of(w_up, me_c), theirs], axis=1)
    w_down_rel = roll_rows(me_y.astype(jnp.int32).reshape(1), w_down)
    here = jnp.stack([lax.axis_index("x"), me_z, me_c]).astype(jnp.int32)
    done = {}
    for colour, pieces in [("second", [z0, z1, z7] + z2), ("first", [x0, x1, x3] + x2)]:
        flat = jnp.concatenate(pieces, axis=0)
        made = jnp.dot(flat[:, :half], w_both, preferred_element_type=f32)
        other = shift(made[:, 2 * slice_h :], "core", 1)
        made = made[:, : 2 * slice_h] + other
        hidden = (jax.nn.silu(made[:, :slice_h]) * made[:, slice_h:]).astype(bf16)
        full = [hidden] + [shift(hidden, "local", -y) for y in range(1, NY)]
        out = jnp.dot(jnp.concatenate(full, axis=1), w_down_rel, preferred_element_type=f32)
        out = out.astype(bf16).astype(f32)
        info = flat[:, half:].astype(f32)
        ids = info[:, :chosen].astype(jnp.int32)
        fixed = info[:, chosen : 2 * chosen] * 256.0 + info[:, 2 * chosen : 3 * chosen]
        scale = jnp.sum(jnp.where(ids == me_expert, fixed, 0.0), axis=1) / 32768.0
        out = (out * scale[:, None]).astype(bf16).reshape(-1, NC, b // NC, slice_d)
        away = lax.dynamic_index_in_dim(out, 1 - me_c, 1, keepdims=False)
        away = shift(away, "core", 1)
        out = place_blocks(here, jnp.array(FIRST if colour == "first" else SECOND, jnp.int32), out, away)
        out = lax.all_to_all(out.reshape((NX, NZ) + out.shape[1:]), "x", 0, 0, tiled=True)
        done[colour] = jnp.sum(out.astype(f32), axis=0).astype(bf16)
    ring = jnp.stack([v.reshape(NZ, NY, rows // 2, slice_d) for v in (done["first"], done["second"])], axis=2)
    ring = lax.all_to_all(ring.reshape(NZ * NY, rows, slice_d), ("z", "local"), 0, 0, tiled=True)
    mixed = jnp.sum(ring.reshape(NZ, NY, rows, slice_d).astype(f32), axis=0).astype(bf16)
    return jnp.concatenate([mixed[d] for d in range(NY)], axis=1)


def solution(mesh):
    fine = Mesh(mesh.devices.reshape(NX, NZ, NC, NY), ("x", "z", "core", "local"))
    node = ("x", "z", "core")
    row = P(node + ("local",), None)
    wide = P(node, None, "local")
    return jax.shard_map(layer, mesh=fine, in_specs=(row, row, row, wide, wide, wide), out_specs=row, check_vma=False)
```
